32 devices in a mesh: ctx: 16 (over z, x, core), ch: 2 (over y).
Axes of the slice: x: 2, y: 2, z: 4, core: 2. Of those that a mesh axis runs over, the one named last changes fastest.
Arguments:
- q_proj: bfloat16 [512, 16384], P('ch', 'ctx'), may hold values from -6 to 6
- k_proj: bfloat16 [512, 16384], P('ch', 'ctx'), may hold values from -6 to 6
- v_proj: bfloat16 [512, 16384], P('ch', 'ctx'), may hold values from -6 to 6
- short_taps: bfloat16 [3, 512, 3], P(None, 'ch'), may hold values from -3.5 to 3.5
- long_filter: float32 [512, 16384], P('ch', 'ctx'), may hold values from -4 to 4
- skip_gain: float32 [512], P('ch'), may hold values from 0.5 to 1.5
- out_weight: bfloat16 [512, 4096], P(None, 'ch'), may hold values from -0.25 to 0.25
Outputs:
- block_out: bfloat16 [16384, 4096], P('ctx', 'ch')
The draws below stay inside these ranges and needn't reach their ends.
All inputs are finite; a program needn't handle non-finite values.
Results may differ from the reference program's by a relative error of at most 0.012.
Values may be sent and summed in bfloat16 or wider, within the bound.
No kernel may reach another device: no remote copies, remote signals or barrier semaphores. Data moves between devices by JAX's collectives and lax.ppermute only.
A program may use at most 128 MiB of HBM per device.

```python
import jax
import jax.numpy as jnp
from jax import lax

D = 4096
CHANNEL_COUNT = 512
SHORT = 3
SEQUENCE_LENGTH = 16384


def draw_long_filter(key, part):
    random_subkeys = jax.random.split(key, 6)
    position_grid = jnp.arange(SEQUENCE_LENGTH, dtype=jnp.float32)[None, :]
    fast_count = 5
    is_fast = jax.random.randint(random_subkeys[0], (CHANNEL_COUNT,), 0, 10) < fast_count
    fast_reach = jax.random.uniform(random_subkeys[1], (CHANNEL_COUNT,), minval=30.0, maxval=50.0)
    slow_rate = jax.random.uniform(random_subkeys[2], (CHANNEL_COUNT,), minval=0.1, maxval=2.0)
    decay_rate = jnp.where(is_fast, 1.0 / fast_reach, slow_rate / SEQUENCE_LENGTH)
    decay_profile = jnp.exp(-decay_rate[:, None] * position_grid)
    spike_location = jax.random.randint(random_subkeys[3], (CHANNEL_COUNT, 3), 1, SEQUENCE_LENGTH)
    spike_mask = jax.random.uniform(random_subkeys[4], (CHANNEL_COUNT, 3), minval=0.5, maxval=0.8)
    for spike_index in range(3):
        mixed_features = position_grid >= spike_location[:, spike_index:spike_index + 1].astype(jnp.float32)
        decay_profile = decay_profile * jnp.where(mixed_features, spike_mask[:, spike_index:spike_index + 1], 1.0)
    energy = jnp.expm1(-2.0 * decay_rate * SEQUENCE_LENGTH) / jnp.expm1(-2.0 * decay_rate)
    rough_part = jnp.clip(jax.random.normal(random_subkeys[5], (CHANNEL_COUNT, SEQUENCE_LENGTH)), -4.0, 4.0)
    return (rough_part * decay_profile / jnp.sqrt(energy)[:, None]).astype(jnp.float32)


def levels(key, dims, cuts, low, top_value):
    loudness, own = 1.0, jax.random.fold_in(key, 6)
    for dim, blocks in cuts:
        steps = jnp.exp(jax.random.uniform(jax.random.fold_in(own, dim), (blocks,), jnp.float32, low / len(cuts), top_value / len(cuts)))
        loudness = loudness * jnp.repeat(steps, dims[dim] // blocks).reshape([-1 if axis == dim else 1 for axis in range(len(dims))])
    return loudness


def gaussian(rng, extent, scale, limit, cuts=(), kind=jnp.bfloat16):
    drawn = scale * jax.random.normal(rng, extent, jnp.float32)
    if cuts:
        drawn = drawn * levels(rng, extent, cuts, -0.22, 0.18)
    return jnp.clip(drawn, -limit, limit).astype(kind)


def setup_inputs(seed: int = 0) -> dict:
    key_list = jax.random.split(jax.random.key(seed), 8)
    return {
        "q_proj": gaussian(key_list[0], (CHANNEL_COUNT, SEQUENCE_LENGTH), 1.0, 6.0, ((0, 2), (1, 16))),
        "k_proj": gaussian(key_list[1], (CHANNEL_COUNT, SEQUENCE_LENGTH), 1.0, 6.0, ((0, 2), (1, 16))),
        "v_proj": gaussian(key_list[2], (CHANNEL_COUNT, SEQUENCE_LENGTH), 1.0, 6.0, ((0, 2), (1, 16))),
        "short_taps": gaussian(key_list[3], (3, CHANNEL_COUNT, SHORT), SHORT ** -0.5, 3.5, ((1, 2),)),
        "long_filter": draw_long_filter(jax.random.fold_in(key_list[7], 71), 0),
        "skip_gain": jnp.clip(0.5 + 1.0 * jax.random.uniform(key_list[5], (CHANNEL_COUNT,), jnp.float32) ** levels(key_list[5], (CHANNEL_COUNT,), ((0, 2),), -0.2, 0.2), 0.5, 1.5),
        "out_weight": gaussian(key_list[6], (CHANNEL_COUNT, D), CHANNEL_COUNT ** -0.5, 0.25, ((1, 2),)),
    }


def causal_filter(signal, weights):
    tap_count = weights.shape[1]
    length = signal.shape[1]
    padded = jnp.pad(signal, ((0, 0), (tap_count - 1, 0)))
    summed = jnp.zeros(signal.shape, jnp.float32)
    for offset in range(tap_count):
        begin_at = tap_count - 1 - offset
        summed = summed + weights[:, offset:offset + 1] * padded[:, begin_at:begin_at + length]
    return summed


def slab_block(pieces):
    query, keys_in, values_in, filter_rows, short_rows, skip_rows = pieces
    q_short = causal_filter(query.astype(jnp.float32), short_rows[:, 0].astype(jnp.float32))
    k_short = causal_filter(keys_in.astype(jnp.float32), short_rows[:, 1].astype(jnp.float32))
    v_short = causal_filter(values_in.astype(jnp.float32), short_rows[:, 2].astype(jnp.float32))
    product_kv = (k_short * v_short).astype(jnp.bfloat16).astype(jnp.float32)
    seq_len = product_kv.shape[1]
    spectrum = jnp.fft.rfft(product_kv, n=2 * seq_len, axis=1) * jnp.fft.rfft(filter_rows, n=2 * seq_len, axis=1)
    long_out = jnp.fft.irfft(spectrum, n=2 * seq_len, axis=1)[:, :seq_len].astype(jnp.float32)
    return (q_short * (long_out + skip_rows[:, None] * product_kv)).astype(jnp.bfloat16)


def reference(q_proj, k_proj, v_proj, short_taps, long_filter, skip_gain, out_weight):
    block_size = 8
    block_count = CHANNEL_COUNT // block_size

    def split_rows(array):
        return array.reshape((block_count, block_size) + array.shape[1:])

    short_rows = jnp.transpose(short_taps, (1, 0, 2))
    gated = lax.map(slab_block, (split_rows(q_proj), split_rows(k_proj), split_rows(v_proj), split_rows(long_filter), split_rows(short_rows), split_rows(skip_gain)))
    gated = gated.reshape(CHANNEL_COUNT, SEQUENCE_LENGTH)
    row_block = min(SEQUENCE_LENGTH, 8192)
    row_groups = gated.reshape(CHANNEL_COUNT, SEQUENCE_LENGTH // row_block, row_block).transpose(1, 0, 2)

    def project(columns):
        return jnp.dot(columns.T, out_weight, preferred_element_type=jnp.float32).astype(jnp.bfloat16)

    projected = lax.map(project, row_groups)
    return projected.reshape(SEQUENCE_LENGTH, D)
```

```python
import functools

import jax
import jax.numpy as jnp
import numpy as np
from jax import lax
from jax.experimental import pallas as pl
from jax.experimental.pallas import tpu as pltpu
from jax.sharding import PartitionSpec as P

LANES = 128
f32, bf16 = jnp.float32, jnp.bfloat16


def split_table(table):
    high = table.astype(jnp.bfloat16)
    low = (table - high.astype(np.float64)).astype(jnp.bfloat16)
    return np.stack([high, low])


def transform_tables(n1):
    shifted = np.arange(n1)[:, None] + 0.25
    angle = -2 * np.pi * shifted * np.arange(n1)[None, :] / n1
    first = split_table(np.concatenate([np.cos(angle), np.sin(angle)], 0))
    twist = -2 * np.pi * shifted * np.arange(LANES)[None, :] / (n1 * LANES)
    lane = np.arange(LANES)
    inner = -2 * np.pi * (lane[:, None] * lane[None, :] % LANES) / LANES
    c, s = np.cos(inner), np.sin(inner)
    return dict(
        first=np.concatenate([first[0], first[1]], 1),
        twist=np.stack([np.cos(twist), np.sin(twist)]).astype(np.float32),
        forward=split_table(np.block([[c, s], [-s, c]])),
        inverse=split_table(np.block([[c, -s], [s, c]]) / LANES),
        last=split_table(np.concatenate([np.cos(angle.T), np.sin(angle.T)], 1) / n1),
    )


def split(x):
    high = x.astype(bf16)
    return high, (x - high.astype(f32)).astype(bf16)


def dot(a, b):
    return lax.dot_general(a, b, (((1,), (0,)), ((), ())), preferred_element_type=f32)


def dot_table(x, table):
    high, low = split(x)
    return dot(high, table[0]) + dot(low, table[0]) + dot(high, table[1])


def rows_by_channel(source, scratch, channels, sources, rows):
    n1 = sources * rows
    for s in range(sources):
        block = source[s].astype(f32)
        for r in range(rows):
            scratch[pl.ds(s * rows + r, channels, stride=n1), :] = block[:, r * LANES : (r + 1) * LANES]


def forward_transform(scratch, first, twist, forward, base, n1, pair):
    x = jnp.concatenate([scratch[pl.ds(base + p * n1, n1), :].astype(bf16) for p in range(pair)], 1)
    a = dot(first[...], jnp.concatenate([x, x], 0))
    tc, ts = twist[0], twist[1]
    out = []
    for p in range(pair):
        re, im = a[:n1, p * LANES : (p + 1) * LANES], a[n1:, p * LANES : (p + 1) * LANES]
        out.append(dot_table(jnp.concatenate([re * tc - im * ts, re * ts + im * tc], 1), forward))
    return out


def spectrum_kernel(h, first, twist, forward, out, scratch, *, channels, sources, rows, pair):
    n1 = sources * rows
    rows_by_channel(h, scratch, channels, sources, rows)

    def body(i, carry):
        base = pl.multiple_of(i * (pair * n1), 8)
        for p, spec in enumerate(forward_transform(scratch, first, twist, forward, base, n1, pair)):
            out[pl.ds(base + p * n1, n1), :] = spec
        return carry

    lax.fori_loop(0, channels // pair, body, 0)


def conv_kernel(u, spectrum, first, twist, forward, inverse, last, out, scratch, *, channels, sources, rows, pair):
    n1 = sources * rows
    rows_by_channel(u, scratch, channels, sources, rows)

    def body(i, carry):
        base = pl.multiple_of(i * (pair * n1), 8)
        tc, ts = twist[0], twist[1]
        highs, lows = [], []
        for p, spec in enumerate(forward_transform(scratch, first, twist, forward, base, n1, pair)):
            other = spectrum[pl.ds(base + p * n1, n1), :]
            xr, xi, hr, hi = spec[:, :LANES], spec[:, LANES:], other[:, :LANES], other[:, LANES:]
            b = dot_table(jnp.concatenate([xr * hr - xi * hi, xr * hi + xi * hr], 1), inverse)
            br, bi = b[:, :LANES], b[:, LANES:]
            high, low = split(jnp.concatenate([br * tc + bi * ts, bi * tc - br * ts], 0))
            highs.append(high)
            lows.append(low)
        high, low = jnp.concatenate(highs, 1), jnp.concatenate(lows, 1)
        y = dot(last[0], high) + dot(last[0], low) + dot(last[1], high)
        for p in range(pair):
            scratch[pl.ds(base + p * n1, n1), :] = y[:, p * LANES : (p + 1) * LANES]
        return carry

    lax.fori_loop(0, channels // pair, body, 0)
    for s in range(sources):
        for r in range(rows):
            piece = scratch[pl.ds(s * rows + r, channels, stride=n1), :]
            out[s, :, r * LANES : (r + 1) * LANES] = piece.astype(out.dtype)


def transform_call(kernel, name, shaped, out_shape, *operands):
    sources, channels, tokens = shaped.shape
    rows = tokens // LANES
    static = dict(channels=channels, sources=sources, rows=rows, pair=2 if channels % 2 == 0 else 1)
    return pl.pallas_call(
        functools.partial(kernel, **static),
        out_shape=out_shape,
        scratch_shapes=[pltpu.VMEM((channels * sources * rows, LANES), f32)],
        name=name,
    )(shaped, *operands)


def passed_along(value, axis, steps):
    count = lax.axis_size(axis)
    return lax.ppermute(value, axis, [(i, i + steps) for i in range(count - steps)])


def short_filter(extended, weights, length):
    span = weights.shape[-1]
    summed = jnp.zeros(extended.shape[:-1] + (length,), f32)
    for offset in range(span):
        begin = span - 1 - offset
        summed = summed + weights[..., offset : offset + 1].astype(f32) * extended[..., begin : begin + length].astype(f32)
    return summed


def local(q_proj, k_proj, v_proj, short_taps, long_filter, skip_gain, out_weight):
    channels, tokens = q_proj.shape
    sources = lax.axis_size("ctx")
    own = channels // sources
    halves = lax.axis_size("ch")
    tables = {name: jnp.asarray(t) for name, t in transform_tables(sources * tokens // LANES).items()}
    n1 = sources * tokens // LANES

    filter_moved = lax.all_to_all(long_filter.astype(bf16).reshape(sources, own, tokens), "ctx", 0, 0)
    stacked = jnp.stack([q_proj, k_proj, v_proj])
    rim = passed_along(stacked[:, :, tokens - short_taps.shape[2] + 1 :], "ctx", 1)
    filtered = short_filter(jnp.concatenate([rim, stacked], axis=2), short_taps, tokens)
    q_short = filtered[0]
    product_kv = (filtered[1] * filtered[2]).astype(bf16)
    signal_moved = lax.all_to_all(product_kv.reshape(sources, own, tokens), "ctx", 0, 0)

    spectrum = transform_call(
        spectrum_kernel, "spectrum", filter_moved, jax.ShapeDtypeStruct((own * n1, 2 * LANES), f32),
        tables["first"], tables["twist"], tables["forward"],
    )
    result = transform_call(
        conv_kernel, "convolve", signal_moved, jax.ShapeDtypeStruct(signal_moved.shape, bf16),
        spectrum, tables["first"], tables["twist"], tables["forward"], tables["inverse"], tables["last"],
    )
    long_out = lax.all_to_all(result, "ctx", 0, 0).reshape(channels, tokens).astype(f32)
    gated = (q_short * (long_out + skip_gain[:, None] * product_kv.astype(f32))).astype(bf16)

    mine = lax.axis_index("ch")
    summed = None
    for step in range(halves):
        piece = gated if step == 0 else lax.ppermute(gated, "ch", [(i, (i + step) % halves) for i in range(halves)])
        owner = (mine - step) % halves
        weights = lax.dynamic_slice_in_dim(out_weight, owner * channels, channels, axis=0)
        part = jnp.einsum("cb,cd->bd", piece, weights, preferred_element_type=f32)
        summed = part if summed is None else summed + part
    return summed.astype(bf16)


def solution(mesh):
    in_specs = (P("ch", "ctx"), P("ch", "ctx"), P("ch", "ctx"), P(None, "ch", None), P("ch", "ctx"), P("ch"), P(None, "ch"))
    return jax.shard_map(local, mesh=mesh, in_specs=in_specs, out_specs=P("ctx", "ch"), check_vma=False)
```

```python
import functools
import math

import jax
import jax.numpy as jnp
import numpy as np
from jax import lax
from jax.experimental import pallas as pl
from jax.experimental.pallas import tpu as pltpu
from jax.sharding import PartitionSpec as P

LANES = 128
GROUP = 8
STEPS = 2
f32, bf16 = jnp.float32, jnp.bfloat16


def split_table(table):
    high = table.astype(jnp.bfloat16)
    low = (table - high.astype(np.float64)).astype(jnp.bfloat16)
    return np.stack([high, low])


def thrice(table, axis):
    high, low = split_table(table)
    return np.concatenate([high, high, low], axis)


def transform_tables(n1):
    shifted = np.arange(n1)[:, None] + 0.25
    angle = -2 * np.pi * shifted * np.arange(n1)[None, :] / n1
    first = split_table(np.concatenate([np.cos(angle), np.sin(angle)], 0))
    twist = -2 * np.pi * shifted * np.arange(LANES)[None, :] / (n1 * LANES)
    lane = np.arange(LANES)
    inner = -2 * np.pi * (lane[:, None] * lane[None, :] % LANES) / LANES
    c, s = np.cos(inner), np.sin(inner)
    return dict(
        first=np.concatenate([first[0], first[1]], 1),
        twist=np.stack([np.cos(twist), np.sin(twist)]).astype(np.float32),
        forward=thrice(np.block([[c, s], [-s, c]]), 0),
        inverse=thrice(np.block([[c, -s], [s, c]]) / LANES, 0),
        last=thrice(np.concatenate([np.cos(angle.T), np.sin(angle.T)], 1) / n1, 1),
    )


def split(x):
    high = x.astype(bf16)
    return high, (x - high.astype(f32)).astype(bf16)


def dot(a, b):
    return lax.dot_general(a, b, (((1,), (0,)), ((), ())), preferred_element_type=f32)


def dot_table(x, table):
    high, low = split(x)
    return dot(jnp.concatenate([high, low, high], 1), table[...])


def rows_by_channel(source, scratch, channels, count, rows, n1, order=None, base=0):
    for s in range(count):
        block = source[s].astype(f32)
        first = (base + s) * rows if order is None else pl.multiple_of(order[base + s] * rows, rows)
        for r in range(rows):
            scratch[pl.ds(first + r, channels, stride=n1), :] = block[:, r * LANES : (r + 1) * LANES]


def groups_of(channels, size):
    return [list(range(i, min(i + size, channels))) for i in range(0, channels, size)]


def forward_transform(planes, first, twist, forward, group, n1):
    tc, ts = twist[0], twist[1]
    stacked = [[] for _ in planes]
    for c in group:
        x = jnp.concatenate([plane[c * n1 : (c + 1) * n1, :].astype(bf16) for plane in planes], 1)
        a = dot(first[...], jnp.concatenate([x, x], 0))
        for p in range(len(planes)):
            re, im = a[:n1, p * LANES : (p + 1) * LANES], a[n1:, p * LANES : (p + 1) * LANES]
            stacked[p].append(jnp.concatenate([re * tc - im * ts, re * ts + im * tc], 1))
    return dot_table(jnp.concatenate(sum(stacked, []), 0), forward)


def start_copies(sources, targets, sems, base=0):
    copies = [pltpu.make_async_copy(x, y, sems.at[base + i]) for i, (x, y) in enumerate(zip(sources, targets))]
    for copy in copies:
        copy.start()
    return copies


def conv_kernel(order, *refs, count, channels, sources, rows):
    arrived, u, tables, out = refs[:count], refs[count], refs[count + 1 : count + 6], refs[count + 6]
    moved, held, first, twist, forward, inverse, last, h_plane, u_plane, sems = refs[count + 7 :]
    n1 = sources * rows
    each = sources // count
    parts = [pl.ds(i * each, each) for i in range(count)]
    inputs = start_copies(list(arrived) + [u.at[p] for p in parts], [moved.at[p] for p in parts] + [held.at[p] for p in parts], sems)
    filled = start_copies(tables, (first, twist, forward, inverse, last), sems, 2 * count)
    for i in range(count):
        inputs[i].wait()
        rows_by_channel(moved.at[parts[i]], h_plane, channels, each, rows, n1, order, i * each)
    for i in range(count):
        inputs[count + i].wait()
        rows_by_channel(held.at[parts[i]], u_plane, channels, each, rows, n1, base=i * each)
    for copy in filled:
        copy.wait()
    tc, ts = twist[0], twist[1]
    for group in groups_of(channels, GROUP):
        both = forward_transform((u_plane, h_plane), first, twist, forward, group, n1)
        spec, other = both[: len(group) * n1], both[len(group) * n1 :]
        xr, xi, hr, hi = spec[:, :LANES], spec[:, LANES:], other[:, :LANES], other[:, LANES:]
        back = dot_table(jnp.concatenate([xr * hr - xi * hi, xr * hi + xi * hr], 1), inverse)
        for pair in groups_of(len(group), 2):
            columns = []
            for p in pair:
                br, bi = back[p * n1 : (p + 1) * n1, :LANES], back[p * n1 : (p + 1) * n1, LANES:]
                high, low = split(jnp.concatenate([br * tc + bi * ts, bi * tc - br * ts], 0))
                columns.append(jnp.concatenate([high, low, high], 0))
            y = dot(last[...], jnp.concatenate(columns, 1))
            for i, p in enumerate(pair):
                u_plane[group[p] * n1 : (group[p] + 1) * n1, :] = y[:, i * LANES : (i + 1) * LANES]
    for s in range(sources):
        for r in range(rows):
            piece = u_plane[pl.ds(s * rows + r, channels, stride=n1), :]
            out[s, :, r * LANES : (r + 1) * LANES] = piece.astype(out.dtype)


def edge_kernel(q, k, v, out, *, width):
    rows = [x[...].astype(f32).T[LANES - width :, :] for x in (q, k, v)]
    rows.append(jnp.zeros((out.shape[0] - 3 * width, out.shape[1]), f32))
    out[...] = jnp.concatenate(rows, 0).astype(out.dtype)


def edges(q, k, v, width):
    channels, tokens = q.shape
    block = pl.BlockSpec((channels, LANES), lambda i: (0, tokens // LANES - 1))
    return pl.pallas_call(
        functools.partial(edge_kernel, width=width),
        grid=(1,),
        in_specs=[block] * 3,
        out_specs=pl.BlockSpec((16, channels), lambda i: (0, 0)),
        out_shape=jax.ShapeDtypeStruct((16, channels), bf16),
        compiler_params=room(8),
        name="edges",
    )(*in_hbm(q, k, v))


def filtered(x, taps, rim, width):
    lane = lax.broadcasted_iota(jnp.int32, x.shape, 1)
    total = taps[:, :1] * x
    for back in range(1, width + 1):
        moved = pltpu.roll(x, back, 1)
        for i in range(back):
            moved = jnp.where(lane == i, rim[:, width - back + i : width - back + i + 1], moved)
        total = total + taps[:, back : back + 1] * moved
    return total


def columns_of(*arrays):
    rows = [x.astype(f32) for x in arrays]
    count = sum(x.shape[0] for x in rows)
    rows.append(jnp.zeros((LANES - count, rows[0].shape[1]), f32))
    return jnp.concatenate(rows, 0).T


def pair_kernel(k, v, taps, rim, out, *, width):
    span = width + 1
    columns = columns_of(rim[...], taps[1], taps[2])
    base = rim.shape[0]
    ks = filtered(k[...].astype(f32), columns[:, base : base + span], columns[:, width : 2 * width], width)
    vs = filtered(v[...].astype(f32), columns[:, base + span : base + 2 * span], columns[:, 2 * width : 3 * width], width)
    out[...] = (ks * vs).astype(out.dtype)


def query_kernel(q, taps, rim, out, *, width):
    columns = columns_of(rim[...], taps[0])
    base = rim.shape[0]
    out[...] = filtered(q[...].astype(f32), columns[:, base : base + width + 1], columns[:, :width], width)


def featurize(kernel, arrays, tap_rows, rim, dtype):
    channels, tokens = arrays[0].shape
    size = channels // STEPS if channels % (STEPS * LANES) == 0 else channels
    rows = pl.BlockSpec((size, tokens), lambda i: (i, 0))
    return pl.pallas_call(
        functools.partial(kernel, width=tap_rows.shape[1] - 1),
        grid=(channels // size,),
        in_specs=[rows] * len(arrays)
        + [
            pl.BlockSpec(tap_rows.shape[:2] + (size,), lambda i: (0, 0, i)),
            pl.BlockSpec((rim.shape[0], size), lambda i: (0, i)),
        ],
        out_specs=rows,
        out_shape=jax.ShapeDtypeStruct((channels, tokens), dtype),
        compiler_params=room(12),
    )(*in_hbm(*arrays), tap_rows, rim)


def pack_kernel(inner_index, *refs, count, inner, own):
    pieces, outs = refs[:count], refs[count:]
    for step in range(inner):
        begin = pl.multiple_of(((inner_index[0] + step) % inner) * own, own)
        for i in range(count):
            outs[step][i] = pieces[i][pl.ds(begin, own), :]


def in_hbm(*values):
    return [pltpu.with_memory_space_constraint(value, pltpu.HBM) for value in values]


def room(mebibytes):
    return pltpu.CompilerParams(vmem_limit_bytes=mebibytes << 20)


def smem():
    return pl.BlockSpec(memory_space=pltpu.SMEM)


def vmem():
    return pl.BlockSpec(memory_space=pltpu.VMEM)


def moved_filter(long_filter, sources, own):
    tokens = long_filter.shape[1]
    inner = max(d for d in range(1, int(math.isqrt(sources)) + 1) if sources % d == 0)
    outer = sources // inner
    group = own * inner
    me = lax.axis_index("ctx")
    me_outer, me_inner = me // inner, me % inner

    def outer_pairs(step):
        return [(i, (i // inner + step) % outer * inner + i % inner) for i in range(sources)]

    def inner_pairs(step):
        return [(i, i // inner * inner + (i % inner + step) % inner) for i in range(sources)]

    pieces = []
    for step in range(outer):
        piece = lax.dynamic_slice_in_dim(long_filter, (me_outer + step) % outer * group, group, 0).astype(bf16)
        pieces.append(piece if step == 0 else lax.ppermute(piece, "ctx", outer_pairs(step)))
    if own % 16 == 0:
        packed = pl.pallas_call(
            functools.partial(pack_kernel, count=outer, inner=inner, own=own),
            in_specs=[smem()] + [vmem()] * outer,
            out_specs=[vmem()] * inner,
            out_shape=[jax.ShapeDtypeStruct((outer, own, tokens), bf16)] * inner,
            compiler_params=room(8),
            name="pack",
        )(me_inner[None].astype(jnp.int32), *pieces)
    else:
        stacked = jnp.stack(pieces)
        packed = [
            lax.dynamic_slice_in_dim(stacked, (me_inner + step) % inner * own, own, 1) for step in range(inner)
        ]
    arrived = [packed[0]] + [lax.ppermute(packed[step], "ctx", inner_pairs(step)) for step in range(1, inner)]
    order = ((me_outer - jnp.arange(outer))[None, :] % outer) * inner + ((me_inner - jnp.arange(inner)) % inner)[:, None]
    return arrived, order.reshape(-1).astype(jnp.int32)


def block(q_proj, k_proj, v_proj, short_taps, long_filter, skip_gain, out_weight):
    channels, tokens = q_proj.shape
    width = short_taps.shape[2] - 1
    tap_rows = jnp.swapaxes(short_taps, 1, 2)
    sources = lax.axis_size("ctx")
    own = channels // sources
    halves = lax.axis_size("ch")
    n1 = sources * tokens // LANES
    tables = {name: jnp.asarray(t) for name, t in transform_tables(n1).items()}

    rim = lax.ppermute(edges(q_proj, k_proj, v_proj, width), "ctx", [(i, i + 1) for i in range(sources - 1)])
    arrived, order = moved_filter(long_filter, sources, own)
    product_kv = featurize(pair_kernel, (k_proj, v_proj), tap_rows, rim, bf16)
    signal_moved = lax.all_to_all(product_kv.reshape(sources, own, tokens), "ctx", 0, 0)
    q_short = featurize(query_kernel, (q_proj,), tap_rows, rim, f32)

    plane = pltpu.VMEM((own * n1, LANES), f32)
    used = [tables[name] for name in ("first", "twist", "forward", "inverse", "last")]
    count = len(arrived)
    result = pl.pallas_call(
        functools.partial(conv_kernel, count=count, channels=own, sources=sources, rows=tokens // LANES),
        in_specs=[smem()] + [pl.BlockSpec(memory_space=pl.ANY)] * (count + 1 + len(used)),
        out_specs=vmem(),
        out_shape=jax.ShapeDtypeStruct(signal_moved.shape, bf16),
        scratch_shapes=[pltpu.VMEM(signal_moved.shape, bf16)] * 2
        + [pltpu.VMEM(t.shape, t.dtype) for t in used]
        + [plane, plane, pltpu.SemaphoreType.DMA((2 * count + len(used),))],
        compiler_params=room(40),
        name="convolve",
    )(order, *arrived, signal_moved, *in_hbm(*used))
    long_out = lax.all_to_all(result, "ctx", 0, 0).reshape(channels, tokens).astype(f32)
    gated = (q_short * (long_out + skip_gain[:, None] * product_kv.astype(f32))).astype(bf16)

    mine = lax.axis_index("ch")
    summed = None
    for step in range(halves):
        piece = gated if step == 0 else lax.ppermute(gated, "ch", [(i, (i + step) % halves) for i in range(halves)])
        owner = (mine - step) % halves
        weights = lax.dynamic_slice_in_dim(out_weight, owner * channels, channels, axis=0)
        part = jnp.einsum("cb,cd->bd", piece, weights, preferred_element_type=f32)
        summed = part if summed is None else summed + part
    return summed.astype(bf16)


def solution(mesh):
    in_specs = (P("ch", "ctx"), P("ch", "ctx"), P("ch", "ctx"), P(None, "ch", None), P("ch", "ctx"), P("ch"), P(None, "ch"))
    return jax.shard_map(block, mesh=mesh, in_specs=in_specs, out_specs=P("ctx", "ch"), check_vma=False)
```

```python
import functools
import math

import jax
import jax.numpy as jnp
import numpy as np
from jax import lax
from jax.experimental import pallas as pl
from jax.experimental.pallas import tpu as pltpu
from jax.sharding import PartitionSpec as P

LANES = 128
GROUP = 8
STEPS = 2
CHUNKS = 4
f32, bf16 = jnp.float32, jnp.bfloat16


def split_table(table):
    high = table.astype(jnp.bfloat16)
    low = (table - high.astype(np.float64)).astype(jnp.bfloat16)
    return np.stack([high, low])


def thrice(table, axis):
    high, low = split_table(table)
    return np.concatenate([high, high, low], axis)


def transform_tables(n1):
    shifted = np.arange(n1)[:, None] + 0.25
    angle = -2 * np.pi * shifted * np.arange(n1)[None, :] / n1
    first = split_table(np.concatenate([np.cos(angle), np.sin(angle)], 0))
    twist = -2 * np.pi * shifted * np.arange(LANES)[None, :] / (n1 * LANES)
    lane = np.arange(LANES)
    inner = -2 * np.pi * (lane[:, None] * lane[None, :] % LANES) / LANES
    c, s = np.cos(inner), np.sin(inner)
    return dict(
        first=np.concatenate([first[0], first[1]], 1),
        twist=np.stack([np.cos(twist), np.sin(twist)]).astype(np.float32),
        forward=thrice(np.block([[c, s], [-s, c]]), 0),
        inverse=thrice(np.block([[c, -s], [s, c]]) / LANES, 0),
        last=thrice(np.concatenate([np.cos(angle.T), np.sin(angle.T)], 1) / n1, 1),
    )


def split(x):
    high = x.astype(bf16)
    return high, (x - high.astype(f32)).astype(bf16)


def dot(a, b):
    return lax.dot_general(a, b, (((1,), (0,)), ((), ())), preferred_element_type=f32)


def dot_table(x, table):
    high, low = split(x)
    return dot(jnp.concatenate([high, low, high], 1), table[...])


def rows_by_channel(source, scratch, channels, count, rows, n1, order=None, base=0):
    for s in range(count):
        block = source[s].astype(f32)
        first = (base + s) * rows if order is None else pl.multiple_of(order[base + s] * rows, rows)
        for r in range(rows):
            scratch[pl.ds(first + r, channels, stride=n1), :] = block[:, r * LANES : (r + 1) * LANES]


def groups_of(channels, size):
    return [list(range(i, min(i + size, channels))) for i in range(0, channels, size)]


def forward_transform(planes, first, twist, forward, group, n1):
    tc, ts = twist[0], twist[1]
    stacked = [[] for _ in planes]
    for c in group:
        x = jnp.concatenate([plane[c * n1 : (c + 1) * n1, :].astype(bf16) for plane in planes], 1)
        a = dot(first[...], jnp.concatenate([x, x], 0))
        for p in range(len(planes)):
            re, im = a[:n1, p * LANES : (p + 1) * LANES], a[n1:, p * LANES : (p + 1) * LANES]
            stacked[p].append(jnp.concatenate([re * tc - im * ts, re * ts + im * tc], 1))
    return dot_table(jnp.concatenate(sum(stacked, []), 0), forward)


def start_copies(sources, targets, sems, base=0):
    copies = [pltpu.make_async_copy(x, y, sems.at[base + i]) for i, (x, y) in enumerate(zip(sources, targets))]
    for copy in copies:
        copy.start()
    return copies


def conv_kernel(order, *refs, count, channels, sources, rows):
    arrived, u, tables, out = refs[:count], refs[count], refs[count + 1 : count + 6], refs[count + 6]
    moved, held, first, twist, forward, inverse, last, h_plane, u_plane, sems = refs[count + 7 :]
    n1 = sources * rows
    each = sources // count
    parts = [pl.ds(i * each, each) for i in range(count)]
    inputs = start_copies(list(arrived) + [u.at[p] for p in parts], [moved.at[p] for p in parts] + [held.at[p] for p in parts], sems)
    filled = start_copies(tables, (first, twist, forward, inverse, last), sems, 2 * count)
    for i in range(count):
        inputs[i].wait()
        rows_by_channel(moved.at[parts[i]], h_plane, channels, each, rows, n1, order, i * each)
    for i in range(count):
        inputs[count + i].wait()
        rows_by_channel(held.at[parts[i]], u_plane, channels, each, rows, n1, base=i * each)
    for copy in filled:
        copy.wait()
    tc, ts = twist[0], twist[1]
    for group in groups_of(channels, GROUP):
        both = forward_transform((u_plane, h_plane), first, twist, forward, group, n1)
        spec, other = both[: len(group) * n1], both[len(group) * n1 :]
        xr, xi, hr, hi = spec[:, :LANES], spec[:, LANES:], other[:, :LANES], other[:, LANES:]
        back = dot_table(jnp.concatenate([xr * hr - xi * hi, xr * hi + xi * hr], 1), inverse)
        for pair in groups_of(len(group), 2):
            columns = []
            for p in pair:
                br, bi = back[p * n1 : (p + 1) * n1, :LANES], back[p * n1 : (p + 1) * n1, LANES:]
                high, low = split(jnp.concatenate([br * tc + bi * ts, bi * tc - br * ts], 0))
                columns.append(jnp.concatenate([high, low, high], 0))
            y = dot(last[...], jnp.concatenate(columns, 1))
            for i, p in enumerate(pair):
                u_plane[group[p] * n1 : (group[p] + 1) * n1, :] = y[:, i * LANES : (i + 1) * LANES]
    for s in range(sources):
        for r in range(rows):
            piece = u_plane[pl.ds(s * rows + r, channels, stride=n1), :]
            out[s, :, r * LANES : (r + 1) * LANES] = piece.astype(out.dtype)


def edge_kernel(q, k, v, out, *, width):
    rows = [x[...].astype(f32).T[LANES - width :, :] for x in (q, k, v)]
    rows.append(jnp.zeros((out.shape[0] - 3 * width, out.shape[1]), f32))
    out[...] = jnp.concatenate(rows, 0).astype(out.dtype)


def edges(q, k, v, width):
    channels, tokens = q.shape
    block = pl.BlockSpec((channels, LANES), lambda i: (0, tokens // LANES - 1))
    return pl.pallas_call(
        functools.partial(edge_kernel, width=width),
        grid=(1,),
        in_specs=[block] * 3,
        out_specs=pl.BlockSpec((16, channels), lambda i: (0, 0)),
        out_shape=jax.ShapeDtypeStruct((16, channels), bf16),
        compiler_params=room(8),
        name="edges",
    )(*in_hbm(q, k, v))


def filtered(x, taps, rim, width):
    lane = lax.broadcasted_iota(jnp.int32, x.shape, 1)
    total = taps[:, :1] * x
    for back in range(1, width + 1):
        moved = pltpu.roll(x, back, 1)
        for i in range(back):
            moved = jnp.where(lane == i, rim[:, width - back + i : width - back + i + 1], moved)
        total = total + taps[:, back : back + 1] * moved
    return total


def columns_of(*arrays):
    rows = [x.astype(f32) for x in arrays]
    count = sum(x.shape[0] for x in rows)
    rows.append(jnp.zeros((LANES - count, rows[0].shape[1]), f32))
    return jnp.concatenate(rows, 0).T


def pair_kernel(k, v, taps, rim, out, *, width):
    span = width + 1
    columns = columns_of(rim[...], taps[1], taps[2])
    base = rim.shape[0]
    ks = filtered(k[...].astype(f32), columns[:, base : base + span], columns[:, width : 2 * width], width)
    vs = filtered(v[...].astype(f32), columns[:, base + span : base + 2 * span], columns[:, 2 * width : 3 * width], width)
    out[...] = (ks * vs).astype(out.dtype)


def query_kernel(q, taps, rim, out, *, width):
    columns = columns_of(rim[...], taps[0])
    base = rim.shape[0]
    out[...] = filtered(q[...].astype(f32), columns[:, base : base + width + 1], columns[:, :width], width)


def featurize(kernel, arrays, tap_rows, rim, dtype):
    channels, tokens = arrays[0].shape
    size = channels // STEPS if channels % (STEPS * LANES) == 0 else channels
    rows = pl.BlockSpec((size, tokens), lambda i: (i, 0))
    return pl.pallas_call(
        functools.partial(kernel, width=tap_rows.shape[1] - 1),
        grid=(channels // size,),
        in_specs=[rows] * len(arrays)
        + [
            pl.BlockSpec(tap_rows.shape[:2] + (size,), lambda i: (0, 0, i)),
            pl.BlockSpec((rim.shape[0], size), lambda i: (0, i)),
        ],
        out_specs=rows,
        out_shape=jax.ShapeDtypeStruct((channels, tokens), dtype),
        compiler_params=room(12),
    )(*in_hbm(*arrays, tap_rows), rim)


def pack_kernel(inner_index, *refs, count, inner, own):
    pieces, outs, sems = refs[:count], refs[count:-1], refs[-1]
    copies = []
    for step in range(inner):
        begin = pl.multiple_of(((inner_index[0] + step) % inner) * own, own)
        sources = [piece.at[pl.ds(begin, own)] for piece in pieces]
        copies += start_copies(sources, [outs[step].at[i] for i in range(count)], sems, step * count)
    for copy in copies:
        copy.wait()


def gate_kernel(y, q_short, product_kv, skip, *refs):
    outs, q_held, kv_held, sems = refs[:-3], refs[-3], refs[-2], refs[-1]
    size = outs[0].shape[1]
    spans = [pl.ds(i * size, size) for i in range(len(outs))]
    waits = []
    for i, span in enumerate(spans):
        sources = [q_short.at[:, span], product_kv.at[:, span]]
        waits.append(start_copies(sources, [q_held.at[:, span], kv_held.at[:, span]], sems, 2 * i))
    gain = columns_of(skip[...])[:, :1]
    for span, out, copies in zip(spans, outs, waits):
        for copy in copies:
            copy.wait()
        mixed = y[:, span].astype(f32) + gain * kv_held[:, span].astype(f32)
        out[...] = (q_held[:, span] * mixed).astype(out.dtype)


def project_kernel(owners, *refs, count, chunk, aliased):
    pieces, weights = refs[:count], refs[count]
    out, held, sems = refs[count + 1 + aliased :]
    channels, size = pieces[0].shape
    rows = pl.ds(chunk * size, size)
    width = min(512, held.shape[1])
    copies = []
    for i in range(held.shape[1] // width):
        span = pl.ds(i * width, width)
        total = None
        for piece, k in zip(pieces, range(count)):
            block = weights[pl.ds(pl.multiple_of(owners[k] * channels, channels), channels), span]
            part = lax.dot_general(piece[...], block, (((0,), (0,)), ((), ())), preferred_element_type=f32)
            total = part if total is None else total + part
        held[:, span] = total.astype(held.dtype)
        copies += start_copies([held.at[:, span]], [out.at[rows, span]], sems, i)
    for copy in copies:
        copy.wait()


def in_hbm(*values):
    return [pltpu.with_memory_space_constraint(value, pltpu.HBM) for value in values]


def room(mebibytes):
    return pltpu.CompilerParams(vmem_limit_bytes=mebibytes << 20)


def smem():
    return pl.BlockSpec(memory_space=pltpu.SMEM)


def vmem():
    return pl.BlockSpec(memory_space=pltpu.VMEM)


def moved_filter(long_filter, sources, own):
    tokens = long_filter.shape[1]
    inner = max(d for d in range(1, int(math.isqrt(sources)) + 1) if sources % d == 0)
    outer = sources // inner
    group = own * inner
    me = lax.axis_index("ctx")
    me_outer, me_inner = me // inner, me % inner

    def outer_pairs(step):
        return [(i, (i // inner + step) % outer * inner + i % inner) for i in range(sources)]

    def inner_pairs(step):
        return [(i, i // inner * inner + (i % inner + step) % inner) for i in range(sources)]

    pieces = []
    for step in range(outer):
        piece = lax.dynamic_slice_in_dim(long_filter, (me_outer + step) % outer * group, group, 0).astype(bf16)
        pieces.append(piece if step == 0 else lax.ppermute(piece, "ctx", outer_pairs(step)))
    if own % 16 == 0:
        packed = pl.pallas_call(
            functools.partial(pack_kernel, count=outer, inner=inner, own=own),
            in_specs=[smem()] + [pl.BlockSpec(memory_space=pl.ANY)] * outer,
            out_specs=[pl.BlockSpec(memory_space=pltpu.HBM)] * inner,
            out_shape=[jax.ShapeDtypeStruct((outer, own, tokens), bf16)] * inner,
            scratch_shapes=[pltpu.SemaphoreType.DMA((outer * inner,))],
            compiler_params=room(8),
            name="pack",
        )(me_inner[None].astype(jnp.int32), *pieces)
    else:
        stacked = jnp.stack(pieces)
        packed = [
            lax.dynamic_slice_in_dim(stacked, (me_inner + step) % inner * own, own, 1) for step in range(inner)
        ]
    arrived = [packed[0]] + [lax.ppermute(packed[step], "ctx", inner_pairs(step)) for step in range(1, inner)]
    order = ((me_outer - jnp.arange(outer))[None, :] % outer) * inner + ((me_inner - jnp.arange(inner)) % inner)[:, None]
    return arrived, order.reshape(-1).astype(jnp.int32)


def block(q_proj, k_proj, v_proj, short_taps, long_filter, skip_gain, out_weight):
    channels, tokens = q_proj.shape
    width = short_taps.shape[2] - 1
    tap_rows = jnp.swapaxes(short_taps, 1, 2)
    sources = lax.axis_size("ctx")
    own = channels // sources
    halves = lax.axis_size("ch")
    n1 = sources * tokens // LANES
    tables = {name: jnp.asarray(t) for name, t in transform_tables(n1).items()}

    rim = lax.ppermute(edges(q_proj, k_proj, v_proj, width), "ctx", [(i, i + 1) for i in range(sources - 1)])
    arrived, order = moved_filter(long_filter, sources, own)
    product_kv = featurize(pair_kernel, (k_proj, v_proj), tap_rows, rim, bf16)
    signal_moved = lax.all_to_all(product_kv.reshape(sources, own, tokens), "ctx", 0, 0)
    q_short = featurize(query_kernel, (q_proj,), tap_rows, rim, f32)

    plane = pltpu.VMEM((own * n1, LANES), f32)
    used = [tables[name] for name in ("first", "twist", "forward", "inverse", "last")]
    count = len(arrived)
    result = pl.pallas_call(
        functools.partial(conv_kernel, count=count, channels=own, sources=sources, rows=tokens // LANES),
        in_specs=[smem()] + [pl.BlockSpec(memory_space=pl.ANY)] * (count + 1 + len(used)),
        out_specs=vmem(),
        out_shape=jax.ShapeDtypeStruct(signal_moved.shape, bf16),
        scratch_shapes=[pltpu.VMEM(signal_moved.shape, bf16)] * 2
        + [pltpu.VMEM(t.shape, t.dtype) for t in used]
        + [plane, plane, pltpu.SemaphoreType.DMA((2 * count + len(used),))],
        compiler_params=room(40),
        name="convolve",
    )(order, *arrived, signal_moved, *in_hbm(*used))
    long_out = lax.all_to_all(result, "ctx", 0, 0).reshape(channels, tokens)
    anywhere = pl.BlockSpec(memory_space=pl.ANY)
    chunks = CHUNKS if tokens % (CHUNKS * LANES) == 0 else 1
    size = tokens // chunks
    gated = pl.pallas_call(
        gate_kernel,
        in_specs=[vmem(), anywhere, anywhere, vmem()],
        out_specs=[vmem()] * chunks,
        out_shape=[jax.ShapeDtypeStruct((channels, size), bf16)] * chunks,
        scratch_shapes=[
            pltpu.VMEM((channels, tokens), f32),
            pltpu.VMEM((channels, tokens), bf16),
            pltpu.SemaphoreType.DMA((2 * chunks,)),
        ],
        compiler_params=room(12),
        name="gate",
    )(long_out, *in_hbm(q_short, product_kv), skip_gain[None, :])

    owners = ((lax.axis_index("ch") - jnp.arange(halves)) % halves).astype(jnp.int32)
    features = out_weight.shape[1]
    pieces = [[piece] for piece in gated]
    for step in range(1, halves):
        for chunk in range(chunks):
            pairs = [(i, (i + step) % halves) for i in range(halves)]
            pieces[chunk].append(lax.ppermute(gated[chunk], "ch", pairs))
    out = ()
    for chunk in range(chunks):
        out = pl.pallas_call(
            functools.partial(project_kernel, count=halves, chunk=chunk, aliased=len(out)),
            in_specs=[smem()] + [vmem()] * (halves + 1) + [anywhere] * len(out),
            out_specs=pl.BlockSpec(memory_space=pltpu.HBM),
            out_shape=jax.ShapeDtypeStruct((tokens, features), bf16),
            scratch_shapes=[pltpu.VMEM((size, features), bf16), pltpu.SemaphoreType.DMA((max(1, features // 512),))],
            input_output_aliases={halves + 2: 0} if out else {},
            compiler_params=room(16),
            name="project",
        )(owners, *pieces[chunk], out_weight, *out)
        out = (out,)
    return out[0]


def solution(mesh):
    in_specs = (P("ch", "ctx"), P("ch", "ctx"), P("ch", "ctx"), P(None, "ch", None), P("ch", "ctx"), P("ch"), P(None, "ch"))
    return jax.shard_map(block, mesh=mesh, in_specs=in_specs, out_specs=P("ctx", "ch"), check_vma=False)
```
